256 devices in a mesh: seq: 64 (over x, z, y_lo), tensor: 4 (over y_hi, core).
Axes of the slice: x: 4, y: 4 (y_hi: 2, y_lo: 2; y = y_hi * 2 + y_lo), z: 8, core: 2. Of those that a mesh axis runs over, the one named last changes fastest.
Arguments:
- hidden: bfloat16 [8192, 1600], P('seq'), may hold values from -6 to 6
- ln_gain: float32 [1600], replicated, may hold values from 0.5 to 1.5
- ln_bias: float32 [1600], replicated, may hold values from -3 to 3
- w_qkv: bfloat16 [1600, 3, 1792], P(None, None, 'tensor'), may hold values from -0.15625 to 0.15625
- b_qkv: float32 [3, 1792], P(None, 'tensor'), may hold values from -3 to 3
- w_out: bfloat16 [1792, 1600], P('tensor'), may hold values from -0.125 to 0.125
- b_out: float32 [1600], replicated, may hold values from -3 to 3
- prefix_kv: bfloat16 [5120, 2, 1792], P('seq', None, 'tensor'), may hold values from -70 to 70
- lengths: int32 [129], replicated, may hold values from 1 to 128, as said below
- req_group: int32 [129], replicated, may hold values from 0 to 3
- block_group: int32 [64], replicated, may hold values from 0 to 3, as said below
Outputs:
- new_hidden: bfloat16 [8192, 1600], P('seq')
- suffix_kv: bfloat16 [8192, 2, 1792], P('seq', None, 'tensor')
The draws below stay inside these ranges and needn't reach their ends.
Inputs may be any that keep to these rules, and one draw needn't show every extreme that they name: `block_group`: each prefix is held by exactly 16 blocks. `lengths`: the longest request has exactly 128 tokens; every multiple of 128 between 0 and 8192 lies strictly inside some request.
All inputs are finite; a program needn't handle non-finite values.
Results may differ from the reference program's by a relative error of at most 0.0038.
The reference program's roundings to bfloat16 on the way (of `normed` and `attn`) count: a program that leaves them out, or rounds other values in their place, can miss the bound.
Values may be sent and summed in bfloat16 or wider, within the bound.
No kernel may reach another device: no remote copies, remote signals or barrier semaphores. Data moves between devices by JAX's collectives and lax.ppermute only.
A program may use at most 128 MiB of HBM per device.

```python
import math
import jax
import jax.numpy as jnp
import numpy as np
from jax import lax

D = 1600
HEADS = 28
HEAD = 64
HID = 1792
PREFIXES = 4
TOK_DEV = 128
TOKENS = 8192
REQS = 129
PTOT = 5120
PB = 80
BLOCKS = 64


def draw_prefix_kv(key, part):
    base_key = jax.random.fold_in(key, 0)
    shape = (PTOT, 2, HID)
    return jax.random.truncated_normal(base_key, -6.0, 6.0, shape, jnp.float32).astype(jnp.bfloat16)


def draw_block_group(key, part):
    return (jax.random.permutation(key, BLOCKS) % PREFIXES).astype(jnp.int32)


def draw_lengths(key, part):
    first_key, second_key, pick_key = jax.random.split(jax.random.fold_in(key, 7), 3)
    count = TOKENS // TOK_DEV
    half = TOK_DEV // 2
    index = jnp.arange(count, dtype=jnp.int32)
    early = jax.random.randint(first_key, (count,), 1, half + 1).astype(jnp.int32)
    later = jax.random.randint(second_key, (count,), half + 1, TOK_DEV).astype(jnp.int32)
    chosen = jax.random.randint(pick_key, (), 0, count - 1).astype(jnp.int32)
    later = jnp.where(index == chosen, half + 1, later)
    early = jnp.where(index == chosen + 1, half + 1, early)
    later = jnp.where(index == chosen + 1, jnp.maximum(later, half + 2), later)
    cuts = jnp.stack([index * TOK_DEV + early, index * TOK_DEV + later], axis=1).reshape(2 * count)
    bounds = jnp.concatenate([jnp.zeros((1,), jnp.int32), cuts, jnp.full((1,), TOKENS, jnp.int32)])
    return (bounds[1:] - bounds[:-1]).astype(jnp.int32)


def with_ends(array, rng, smallest, largest):
    longest = array.shape.index(max(array.shape))
    spots = []
    for shift in (0, 1):
        where = [jax.random.randint(jax.random.fold_in(rng, axis), (), 0, length) for axis, length in enumerate(array.shape)]
        where[longest] = (where[longest] + shift) % array.shape[longest]
        spots.append(tuple(where))
    return array.at[spots[0]].set(smallest).at[spots[1]].set(largest)


def steps_of(key, shape, pieces, smallest, high):
    level, own = 1.0, jax.random.fold_in(key, 6)
    for axis_at, parts in pieces:
        heights = jnp.exp(jax.random.uniform(jax.random.fold_in(own, axis_at), (parts,), jnp.float32, smallest / len(pieces), high / len(pieces)))
        level = level * jnp.repeat(heights, shape[axis_at] // parts).reshape([-1 if axis == axis_at else 1 for axis in range(len(shape))])
    return level


def rank_bounds(number_of, lean):
    portions = [(1 << 20) // math.isqrt(standing ** lean) + 1 for standing in range(1, number_of + 1)]
    scale = 1 + sum(portions) // (1 << 30)
    return np.cumsum(np.array([max(1, weight // scale) for weight in portions]))


def skewed_ids(own_key, shape, number_of, skew):
    listing = rank_bounds(number_of, skew)
    lot = jax.random.randint(jax.random.fold_in(own_key, 1), shape, 0, int(listing[number_of - 1]))
    rank = jnp.searchsorted(jnp.asarray(listing, jnp.int32), lot, side="right")
    return jax.random.permutation(jax.random.fold_in(own_key, 2), number_of)[rank].astype(jnp.int32)


def gaussian(rng, dims, width, reach, cuts=(), kind=jnp.bfloat16):
    result = width * jax.random.normal(rng, dims, jnp.float32)
    if cuts:
        result = result * steps_of(rng, dims, cuts, -0.22, 0.18)
    return jnp.clip(result, -reach, reach).astype(kind)


def setup_inputs(seed: int = 0) -> dict:
    key_of = jax.random.split(jax.random.key(seed), 12)
    hidden = gaussian(key_of[0], (TOKENS, D), 1.0, 6.0, ((0, 64),))
    ln_gain = jnp.clip(1.0 + 0.1 * jax.random.normal(key_of[1], (D,), jnp.float32), 0.5, 1.5)
    ln_bias = gaussian(key_of[2], (D,), 0.5, 3.0, (), jnp.float32)
    w_qkv = gaussian(key_of[3], (D, 3, HID), D ** -0.5, 0.15625, ((2, 4),))
    b_qkv = gaussian(key_of[4], (3, HID), 0.5, 3.0, ((1, 4),), jnp.float32)
    w_out = gaussian(key_of[5], (HID, D), HID ** -0.5, 0.125, ((0, 4),))
    b_out = gaussian(key_of[6], (D,), 0.5, 3.0, (), jnp.float32)
    prefix_kv = draw_prefix_kv(jax.random.fold_in(key_of[11], 71), 0)
    lengths = draw_lengths(jax.random.fold_in(key_of[11], 71), 0)
    req_group = with_ends(skewed_ids(key_of[9], (REQS,), PREFIXES, 2), jax.random.fold_in(key_of[9], 3), 0, PREFIXES - 1).astype(jnp.int32)
    block_group = draw_block_group(jax.random.fold_in(key_of[11], 71), 0)
    return {"hidden": hidden, "ln_gain": ln_gain, "ln_bias": ln_bias, "w_qkv": w_qkv, "b_qkv": b_qkv, "w_out": w_out, "b_out": b_out, "prefix_kv": prefix_kv, "lengths": lengths, "req_group": req_group, "block_group": block_group}


def request_of(positions, lengths):
    ends = jnp.cumsum(lengths)
    return lax.optimization_barrier(jnp.sum((ends[None, :] <= positions[:, None]).astype(jnp.int32), axis=1)).astype(jnp.int32)

def group_of(requests, req_group):
    index = jnp.arange(req_group.shape[0], dtype=jnp.int32)
    return lax.optimization_barrier(jnp.sum(jnp.where(requests[:, None] == index[None, :], req_group[None, :], 0), axis=1)).astype(jnp.int32)

def reference(hidden, ln_gain, ln_bias, w_qkv, b_qkv, w_out, b_out, prefix_kv, lengths, req_group, block_group):
    resid = hidden.astype(jnp.float32)
    center = lax.optimization_barrier(jnp.mean(resid, axis=1, keepdims=True))
    spread = lax.optimization_barrier(jnp.mean((resid - center) ** 2, axis=1, keepdims=True))
    normed = ((resid - center) * lax.rsqrt(spread + 1e-05) * ln_gain + ln_bias).astype(jnp.bfloat16)
    qkv = jnp.einsum('td,dch->tch', normed.astype(jnp.float32), w_qkv.astype(jnp.float32)) + b_qkv.astype(jnp.float32)
    qkv = qkv.astype(jnp.bfloat16)
    suffix_kv = qkv[:, 1:3]
    scale = 1.0 / HEAD ** 0.5
    positions = jnp.arange(TOKENS, dtype=jnp.int32)
    requests = request_of(positions, lengths)
    groups = group_of(requests, req_group)
    query_all = qkv[:, 0].astype(jnp.float32).reshape(TOKENS // TOK_DEV, TOK_DEV, HEADS, HEAD)
    zeros_kv = jnp.zeros((TOK_DEV, 2, HID), jnp.bfloat16)
    padded_kv = jnp.concatenate([zeros_kv, suffix_kv], axis=0).astype(jnp.float32)
    padded_req = jnp.concatenate([jnp.full((TOK_DEV,), -1, jnp.int32), requests]).astype(jnp.int32)
    key_blocks = prefix_kv[:, 0].astype(jnp.float32).reshape(BLOCKS, PB, HEADS, HEAD)
    val_blocks = prefix_kv[:, 1].astype(jnp.float32).reshape(BLOCKS, PB, HEADS, HEAD)

    def one_block(number):
        start = (number * TOK_DEV).astype(jnp.int32)
        query_heads = query_all[number]
        q_req = lax.dynamic_slice_in_dim(requests, start, TOK_DEV, 0)
        q_group = lax.dynamic_slice_in_dim(groups, start, TOK_DEV, 0)
        q_pos = start + jnp.arange(TOK_DEV, dtype=jnp.int32)
        window = lax.dynamic_slice_in_dim(padded_kv, start, 2 * TOK_DEV, 0)
        k_req = lax.dynamic_slice_in_dim(padded_req, start, 2 * TOK_DEV, 0)
        k_pos = start - TOK_DEV + jnp.arange(2 * TOK_DEV, dtype=jnp.int32)
        alive = (k_req[None, :] == q_req[:, None]) & (k_pos[None, :] <= q_pos[:, None])
        keys_win = window[:, 0].reshape(2 * TOK_DEV, HEADS, HEAD)
        vals_win = window[:, 1].reshape(2 * TOK_DEV, HEADS, HEAD)
        scores = jnp.einsum('qhe,khe->qhk', query_heads, keys_win) * scale
        scores = jnp.where(alive[:, None, :], scores, -1e+30)
        top_s = lax.optimization_barrier(jnp.max(scores, axis=2))
        prob_s = jnp.exp(scores - top_s[:, :, None])
        den_s = lax.optimization_barrier(jnp.sum(prob_s, axis=2))
        num_s = jnp.einsum('qhk,khe->qhe', prob_s.astype(jnp.bfloat16).astype(jnp.float32), vals_win)
        scores_p = jnp.einsum('qhe,bkhe->qhbk', query_heads, key_blocks) * scale
        live_p = q_group[:, None] == block_group[None, :]
        scores_p = jnp.where(live_p[:, None, :, None], scores_p, -1e+30)
        top_b = lax.optimization_barrier(jnp.max(scores_p, axis=3))
        prob_p = jnp.where(live_p[:, None, :, None], jnp.exp(scores_p - top_b[:, :, :, None]), 0.0)
        den_b = lax.optimization_barrier(jnp.sum(prob_p, axis=3))
        num_b = jnp.einsum('qhbk,bkhe->qhbe', prob_p.astype(jnp.bfloat16).astype(jnp.float32), val_blocks)
        top_p = lax.optimization_barrier(jnp.max(top_b, axis=2))
        weight_b = jnp.exp(top_b - top_p[:, :, None])
        num_p = lax.optimization_barrier(jnp.sum(num_b * weight_b[:, :, :, None], axis=2))
        den_p = lax.optimization_barrier(jnp.sum(den_b * weight_b, axis=2))
        highest = jnp.maximum(top_p, top_s)
        weight_p = jnp.exp(top_p - highest)
        weight_s = jnp.exp(top_s - highest)
        numer = num_p * weight_p[:, :, None] + num_s * weight_s[:, :, None]
        denom = den_p * weight_p + den_s * weight_s
        return (numer / denom[:, :, None]).astype(jnp.bfloat16).reshape(TOK_DEV, HID)
    attn = lax.map(one_block, jnp.arange(TOKENS // TOK_DEV, dtype=jnp.int32)).reshape(TOKENS, HID)
    projected = jnp.dot(attn, w_out, preferred_element_type=jnp.float32)
    new_hidden = (resid + projected + b_out).astype(jnp.bfloat16)
    return (new_hidden, suffix_kv)
```

```python
import functools

import jax
import jax.numpy as jnp
from jax import lax
from jax.experimental import pallas as pl
from jax.experimental.pallas import tpu as pltpu
from jax.sharding import Mesh, PartitionSpec as P

HEAD = 64
NX, NZ, NY = 4, 8, 2
NEG = -1e30
SEQ = ("x", "z", "yl")
TEN = ("yh", "c")
VMEM = pltpu.VMEM
F32, BF16 = jnp.float32, jnp.bfloat16


def ring(n, d):
    return [(i, (i + d) % n) for i in range(n)]


def vspec():
    return pl.BlockSpec(memory_space=pltpu.VMEM)


def sspec():
    return pl.BlockSpec(memory_space=pltpu.SMEM)


def split3(value):
    hi = value.astype(BF16)
    rest = value - hi.astype(F32)
    mid = rest.astype(BF16)
    return hi, mid, (rest - mid.astype(F32)).astype(BF16)


def prefix_kernel(nq, nkv, sizes, first, last, *refs):
    refs = list(refs)
    bg_ref, qg_ref = refs[:2]
    q_refs = refs[2 : 2 + nq]
    kv_refs = refs[2 + nq : 2 + nq + nkv]
    rest = refs[2 + nq + nkv :]
    if not first:
        acc_in, st_in = rest[:2]
        rest = rest[2:]
    if last:
        packs = rest[:nq]
        rest = rest[nq:]
        acc, stat = rest
    else:
        acc, stat = rest
    heads = q_refs[0].shape[0] // HEAD
    wide = 256
    per = wide // 128
    biases = []
    for jj in range(nq // per):
        row = qg_ref[:, jj * wide : (jj + 1) * wide]
        biases.append(
            [jnp.where(row == bg_ref[b], 0.0, NEG) for b in range(sum(sizes) // 80)]
        )

    def head(h, _):
        rows = pl.ds(pl.multiple_of(h * HEAD, HEAD), HEAD)
        kv = jnp.concatenate([r[h] for r in kv_refs], axis=0)
        for jj in range(nq // per):
            cols = pl.ds(jj * wide, wide)
            q = jnp.concatenate([q_refs[jj * per + i][rows, :] for i in range(per)], axis=1)
            q = jnp.concatenate([q, jnp.zeros_like(q)], axis=0)
            s = jnp.dot(kv, q, preferred_element_type=F32)
            parts = [
                s[80 * b : 80 * b + 80] + biases[jj][b] for b in range(sum(sizes) // 80)
            ]
            s = jnp.concatenate(parts, axis=0)
            top = jnp.max(s, axis=0, keepdims=True)
            if not first:
                old = st_in[0, pl.ds(h, 1), cols]
                top = jnp.maximum(top, old)
            p = jnp.exp(s - top)
            den = jnp.sum(p, axis=0, keepdims=True)
            num = lax.dot_general(
                kv, p.astype(BF16), (((0,), (0,)), ((), ())), preferred_element_type=F32
            )[HEAD:]
            if not first:
                alpha = jnp.exp(old - top)
                den = den + alpha * st_in[1, pl.ds(h, 1), cols]
                num = num + alpha * acc_in[rows, cols]
            stat[0, pl.ds(h, 1), cols] = top
            stat[1, pl.ds(h, 1), cols] = den
            if last:
                for i in range(per):
                    packs[jj * per + i][rows, :] = num[:, i * 128 : i * 128 + 128].astype(BF16)
            else:
                acc[rows, cols] = num
        return 0

    lax.fori_loop(0, heads, head, 0)
    if last:
        stat[0, 7:8, :] = jnp.zeros_like(stat[0, 7:8, :])
        stat[1, 7:8, :] = jnp.zeros_like(stat[1, 7:8, :])
        both = jnp.concatenate([stat[0], stat[1]], axis=0)
        for i in range(nq):
            pieces = split3(both[:, i * 128 : i * 128 + 128])
            for k in range(3):
                packs[i][448 + 16 * k : 464 + 16 * k, :] = pieces[k]


def prefix_call(groups, qg, qs, kvs, state, last):
    sizes = [a.shape[1] for a in kvs]
    nq = len(qs)
    width = qs[0].shape[0]
    tot = nq * 128
    first = state is None
    acc_t = jax.ShapeDtypeStruct((width, tot), F32)
    stat_t = jax.ShapeDtypeStruct((2, 8, tot), F32)
    keys = sum(sizes)
    ops = [groups, qg, *qs, *kvs] + ([] if first else list(state))
    scratch = []
    if last:
        out = [jax.ShapeDtypeStruct((width + 48, 128), BF16)] * nq
        scratch = [pltpu.VMEM((8, 128), F32), pltpu.VMEM((2, 8, tot), F32)]
    else:
        out = [acc_t, stat_t]
    return pl.pallas_call(
        functools.partial(prefix_kernel, nq, len(kvs), sizes, first, last),
        out_shape=out,
        in_specs=[sspec()] + [vspec()] * (len(ops) - 1),
        out_specs=[vspec()] * len(out),
        scratch_shapes=scratch,
        compiler_params=pltpu.CompilerParams(vmem_limit_bytes=40 << 20),
        cost_estimate=pl.CostEstimate(
            flops=4 * 128 * keys * tot * 7,
            transcendentals=keys * tot * 7,
            bytes_accessed=keys * 7 * 256 + tot * 448 * 10,
        ),
        name="prefix_attn",
    )(*ops)


def suffix_kernel(q_ref, prev_ref, own_ref, bias_ref, num_ref, stat_ref):
    heads = q_ref.shape[0] // HEAD
    bias = bias_ref[...]
    stat_ref[...] = jnp.zeros_like(stat_ref)

    def head(h, _):
        rows = pl.ds(pl.multiple_of(h * HEAD, HEAD), HEAD)
        kv = jnp.concatenate([prev_ref[h], own_ref[h]], axis=0)
        q = q_ref[rows, :]
        q = jnp.concatenate([q, jnp.zeros_like(q)], axis=0)
        s = jnp.dot(kv, q, preferred_element_type=F32) + bias
        top = jnp.max(s, axis=0, keepdims=True)
        p = jnp.exp(s - top)
        num = lax.dot_general(
            kv, p.astype(BF16), (((0,), (0,)), ((), ())), preferred_element_type=F32
        )
        num_ref[rows, :] = num[HEAD:]
        stat_ref[0, pl.ds(h, 1), :] = top
        stat_ref[1, pl.ds(h, 1), :] = jnp.sum(p, axis=0, keepdims=True)
        return 0

    lax.fori_loop(0, heads, head, 0)


def suffix_call(q, prev, own, bias):
    return pl.pallas_call(
        suffix_kernel,
        out_shape=[jax.ShapeDtypeStruct(q.shape, F32), jax.ShapeDtypeStruct((2, 8, 128), F32)],
        in_specs=[vspec()] * 4,
        out_specs=[vspec()] * 2,
        cost_estimate=pl.CostEstimate(
            flops=4 * 128 * 256 * 128 * 7, transcendentals=256 * 128 * 7, bytes_accessed=900000
        ),
        name="suffix_attn",
    )(q, prev, own, bias)


def merge_kernel(core_ref, p0, p1, p2, p3, num_s, stat_s, w_ref, keep_ref, send_ref, attn, proj):
    packs = (p0, p1, p2, p3)
    heads = num_s.shape[0] // HEAD
    tops, dens = [], []
    for r in packs:
        both = (
            r[448:464, :].astype(F32) + r[464:480, :].astype(F32) + r[480:496, :].astype(F32)
        )
        tops.append(both[:8])
        dens.append(both[8:])
    tops.append(stat_s[0])
    dens.append(stat_s[1])
    high = functools.reduce(jnp.maximum, tops)
    weights = [jnp.exp(t - high) for t in tops]
    total = sum(d * w for d, w in zip(dens, weights))
    for h in range(heads):
        rows = slice(h * HEAD, h * HEAD + HEAD)
        num = num_s[rows, :] * weights[4][h : h + 1]
        for r, w in zip(packs, weights):
            num = num + r[rows, :].astype(F32) * w[h : h + 1]
        attn[rows, :] = (num / total[h : h + 1]).astype(BF16)
    proj[...] = lax.dot_general(
        attn[...], w_ref[...], (((0,), (0,)), ((), ())), preferred_element_type=F32
    )
    core = core_ref[0]
    keep_ref[...] = proj[pl.ds(pl.multiple_of(core * 64, 64), 64), :]
    send_ref[...] = proj[pl.ds(pl.multiple_of((1 - core) * 64, 64), 64), :].astype(BF16)


def merge_call(core, packs, num_s, stat_s, w_out):
    cols = w_out.shape[1]
    return pl.pallas_call(
        merge_kernel,
        out_shape=[jax.ShapeDtypeStruct((64, cols), F32), jax.ShapeDtypeStruct((64, cols), BF16)],
        in_specs=[sspec()] + [vspec()] * 7,
        out_specs=[vspec()] * 2,
        scratch_shapes=[pltpu.VMEM((448, 128), BF16), pltpu.VMEM((128, cols), F32)],
        cost_estimate=pl.CostEstimate(
            flops=2 * 128 * 448 * cols, transcendentals=0, bytes_accessed=2500000
        ),
        name="merge_project",
    )(core, *packs, num_s, stat_s, w_out)


def heads_first(pair):
    rows, _, width = pair.shape
    heads = width // HEAD
    return pair.reshape(rows, 2, heads, HEAD).transpose(2, 0, 1, 3).reshape(heads, rows, 2 * HEAD)


def body(
    hidden, ln_gain, ln_bias, w_qkv, b_qkv, w_out, b_out, prefix_kv, lengths, req_group, block_group
):
    xi, zi, yi = lax.axis_index("x"), lax.axis_index("z"), lax.axis_index("yl")
    core = lax.axis_index("c")
    rank = (xi * NZ + zi) * NY + yi
    toks = hidden.shape[0]
    index = jnp.arange(toks, dtype=jnp.int32)

    own = heads_first(prefix_kv)
    other = lax.ppermute(own, "yl", ring(NY, 1))
    start = jnp.concatenate([own, other], axis=1)
    got, order = [start], [0]
    fwd = bwd = start
    for step in range(1, NZ // 2):
        fwd = lax.ppermute(fwd, "z", ring(NZ, 1))
        bwd = lax.ppermute(bwd, "z", ring(NZ, -1))
        got += [fwd, bwd]
        order += [-step, step]
    fwd = lax.ppermute(fwd[:, :80], "z", ring(NZ, 1))
    bwd = lax.ppermute(bwd[:, 80:], "z", ring(NZ, -1))
    got += [fwd, bwd]
    names = []
    for off in order:
        names += [((zi + off) % NZ) * NY + yi, ((zi + off) % NZ) * NY + 1 - yi]
    far = ((zi + NZ // 2) % NZ) * NY
    names += [far + yi, far + 1 - yi]
    names = jnp.stack(names) + xi * (NZ * NY)
    slots = jnp.arange(block_group.shape[0], dtype=jnp.int32)
    groups = jnp.sum(
        jnp.where(names[:, None] == slots[None, :], block_group[None, :], 0), axis=1
    ).astype(jnp.int32)

    resid = hidden.astype(F32)
    center = jnp.mean(resid, axis=1, keepdims=True)
    spread = jnp.mean((resid - center) ** 2, axis=1, keepdims=True)
    normed = ((resid - center) * lax.rsqrt(spread + 1e-05) * ln_gain + ln_bias).astype(BF16)
    qkv = jnp.einsum("td,dch->tch", normed, w_qkv, preferred_element_type=F32) + b_qkv
    qkv = qkv.astype(BF16)
    suffix_kv = qkv[:, 1:3]
    query = (qkv[:, 0] * (1.0 / HEAD**0.5)).astype(BF16).T
    mine = heads_first(suffix_kv)
    queries = [query] + [lax.ppermute(query, "x", ring(NX, d)) for d in range(1, NX)]
    line = [(i - 1, i) for i in range(1, NX * NZ * NY)]
    earlier = lax.ppermute(mine, SEQ, line)

    r_index = jnp.arange(lengths.shape[0], dtype=jnp.int32)
    ends = jnp.sum(jnp.where(r_index[:, None] <= r_index[None, :], lengths[:, None], 0), axis=0)
    begins = ends - lengths

    def held(pos):
        return (begins[:, None] <= pos[None, :]) & (pos[None, :] < ends[:, None])

    q_ranks = jnp.stack([(((xi - d) % NX) * NZ + zi) * NY + yi for d in range(NX)])
    all_pos = (q_ranks[:, None] * toks + index[None, :]).reshape(-1)
    q_group = jnp.sum(jnp.where(held(all_pos), req_group[:, None], 0), axis=0, keepdims=True)
    q_pos = rank * toks + index
    k_pos = (rank - 1) * toks + jnp.arange(2 * toks, dtype=jnp.int32)
    q_first = jnp.sum(jnp.where(held(q_pos), begins[:, None], 0), axis=0)
    alive = (k_pos[:, None] <= q_pos[None, :]) & (k_pos[:, None] >= q_first[None, :])
    bias = jnp.where(alive, 0.0, NEG).astype(F32)

    num_s, stat_s = suffix_call(query, earlier, mine, bias)
    state = prefix_call(groups[:10], q_group, queries, got[:5], None, False)
    state = prefix_call(groups[10:14], q_group, queries, got[5:7], state, False)
    packs = prefix_call(groups[14:], q_group, queries, got[7:], state, True)
    packs = [packs[0]] + [lax.ppermute(packs[d], "x", ring(NX, -d)) for d in range(1, NX)]
    keep, send = merge_call(core.reshape(1).astype(jnp.int32), packs, num_s, stat_s, w_out)
    chip = (keep + lax.ppermute(send, "c", ring(2, 1)).astype(F32)).astype(BF16)
    chip2 = lax.ppermute(chip, "yh", ring(2, 1))
    part = lax.dynamic_slice_in_dim(hidden, core * 64, 64, 0).astype(F32) + b_out
    half = (part + (chip.astype(F32) + chip2.astype(F32))).astype(BF16)
    half2 = lax.ppermute(half, "c", ring(2, 1))
    new_hidden = jnp.concatenate(
        [jnp.where(core == 0, half, half2), jnp.where(core == 0, half2, half)], axis=0
    )
    return (new_hidden, suffix_kv)


def solution(mesh):
    fine = Mesh(mesh.devices.reshape(NX, NZ, NY, 2, 2), SEQ + TEN)
    placed = (
        P(SEQ, None),
        P(),
        P(),
        P(None, None, TEN),
        P(None, TEN),
        P(TEN, None),
        P(),
        P(SEQ, None, TEN),
        P(),
        P(),
        P(),
    )
    return jax.shard_map(
        body,
        mesh=fine,
        in_specs=placed,
        out_specs=(P(SEQ, None), P(SEQ, None, TEN)),
        check_vma=False,
    )
```
